32 devices in a mesh: patch: 2 (over y), exp: 4 (over z), strip: 2 (over x), band: 2 (over core).
Axes of the slice: x: 2, y: 2, z: 4, core: 2. Of those that a mesh axis runs over, the one named last changes fastest.
Arguments:
- images: float32 [64, 64, 512], P(('patch', 'exp'), 'strip', 'band'), parts along dimension 0, may hold values from -80 to 80
- valid_mask: int32 [64, 64, 512], P(('patch', 'exp'), 'strip', 'band'), parts along dimension 0, may hold values from 0 to 1, as said below
- basis_index: int32 [64, 4, 2], P(('patch', 'exp'), 'strip'), parts along dimension 0, may hold values from 0 to 15
- match_index: int32 [64, 4, 2], P(('patch', 'exp'), 'strip'), parts along dimension 0, may hold values from 0 to 15
- psf_bank: float32 [16, 81], replicated, may hold values from 0.05 to 1
Outputs:
- coadd_image: float32 [128, 512], P(('patch', 'strip'), 'band'), parts along dimension 0
- difference: float32 [64, 64, 512], P(('patch', 'exp'), 'strip', 'band'), parts along dimension 0
The draws below stay inside these ranges and needn't reach their ends.
There are 2 independent parts, one for each index of `patch`. The reference program is written for one: setup_inputs(seed, part) draws one part's arguments, and reference() takes and returns one part's arrays. A program takes and returns all parts, laid end to end along the dimension named above; an argument that names none is the same for every part. Nothing has to cross between parts.
Inputs may be any that keep to these rules, and one draw needn't show every extreme that they name: `valid_mask`: one marks a valid pixel of that exposure.
All inputs are finite; a program needn't handle non-finite values.
Results may differ from the reference program's by a relative error of at most 0.0003.
Values sent between devices are 32-bit elements; how exact they have to be, the bound alone decides.
No kernel may reach another device: no remote copies, remote signals or barrier semaphores. Data moves between devices by JAX's collectives and lax.ppermute only.
A program may use at most 128 MiB of HBM per device.

```python
import math
import jax
import jax.numpy as jnp
from jax import lax

TILE_ROWS = 16
KERNEL = 9
BASES = 16
EXPOSURES = 32
HEIGHT = 64
WIDTH = 512
TILES = 4


def stack_bits(key):
    shape_all = (EXPOSURES, HEIGHT, WIDTH)
    valid_bits = jax.random.randint(jax.random.fold_in(key, 101), shape_all, 0, 10)
    valid_mask = (valid_bits < 9).astype(jnp.int32)
    hit_bits = jax.random.randint(jax.random.fold_in(key, 102), shape_all, 0, 100)
    return (valid_mask, hit_bits)


def blob_field(key, salt_base, rate_permille):
    block_side = 16
    coarse_shape = (EXPOSURES, HEIGHT // block_side + 2, WIDTH // block_side + 2)
    hit_draw = jax.random.randint(jax.random.fold_in(key, salt_base), coarse_shape, 0, 1000)
    amplitude = 20.0 + 30.0 * jax.random.uniform(jax.random.fold_in(key, salt_base + 1), coarse_shape, jnp.float32)
    coarse_field = jnp.where(hit_draw < rate_permille, amplitude, 0.0)
    shift_rows = jax.random.randint(jax.random.fold_in(key, salt_base + 2), (EXPOSURES, 1, 1), 0, block_side)
    shift_cols = jax.random.randint(jax.random.fold_in(key, salt_base + 3), (EXPOSURES, 1, 1), 0, block_side)
    row_block = (jnp.arange(HEIGHT, dtype=jnp.int32)[None, :, None] + shift_rows) // block_side
    col_block = (jnp.arange(WIDTH, dtype=jnp.int32)[None, None, :] + shift_cols) // block_side
    exposure_ids = jnp.arange(EXPOSURES, dtype=jnp.int32)[:, None, None]
    return coarse_field[exposure_ids, row_block, col_block]


def draw_valid_mask(key, part):
    return stack_bits(key)[0]


def draw_images(key, part):
    shape_all = (EXPOSURES, HEIGHT, WIDTH)
    valid_mask, hit_bits = stack_bits(key)
    sky_scene = 2.0 * jax.random.truncated_normal(jax.random.fold_in(key, 103), -4.0, 4.0, (HEIGHT, WIDTH), jnp.float32)
    read_noise = 0.5 * jax.random.truncated_normal(jax.random.fold_in(key, 104), -4.0, 4.0, shape_all, jnp.float32)
    cosmic = 8.0 + 8.0 * jax.random.uniform(jax.random.fold_in(key, 105), shape_all, jnp.float32)
    bright_blobs = blob_field(key, 201, 15)
    dark_blobs = blob_field(key, 301, 8)
    outlier = jnp.where(hit_bits == 0, 6.0, 0.0) - jnp.where(hit_bits == 1, 6.0, 0.0)
    artifacts = outlier + bright_blobs - dark_blobs
    images = sky_scene[None] + read_noise + jnp.where(valid_mask == 0, cosmic, artifacts)
    return jnp.clip(images, -80.0, 80.0).astype(jnp.float32)


def set_ends(array, stream_key, least, top_value):
    place = [jax.random.randint(jax.random.fold_in(stream_key, axis), (), 0, length) for axis, length in enumerate(array.shape)]
    longest = array.shape.index(max(array.shape))
    neighbour = place[:longest] + [(place[longest] + 1) % array.shape[longest]] + place[longest + 1:]
    return array.at[tuple(place)].set(least).at[tuple(neighbour)].set(top_value)


def setup_inputs(seed: int = 0, part: int = 0) -> dict:
    arg_keys = jax.random.split(jax.random.key(seed), 6)
    own_keys = jax.random.split(jax.random.fold_in(arg_keys[5], part), 6)
    return {
        "images": draw_images(jax.random.fold_in(jax.random.fold_in(arg_keys[5], part), 71), part),
        "valid_mask": draw_valid_mask(jax.random.fold_in(jax.random.fold_in(arg_keys[5], part), 71), part),
        "basis_index": set_ends(jax.random.randint(own_keys[2], (EXPOSURES, TILES, 2), 0, BASES), jax.random.fold_in(own_keys[2], 1), 0, BASES - 1).astype(jnp.int32),
        "match_index": set_ends(jax.random.randint(own_keys[3], (EXPOSURES, TILES, 2), 0, BASES), jax.random.fold_in(own_keys[3], 1), 0, BASES - 1).astype(jnp.int32),
        "psf_bank": jnp.clip(jnp.exp(jax.random.uniform(arg_keys[4], (BASES, KERNEL * KERNEL), jnp.float32, math.log(0.05), math.log(1.0))), 0.05, 1.0),
    }


sentinel = 1.0e30


def vary_conv(padded, kernels, blend_map):
    row_count = kernels.shape[-3]
    col_count = blend_map.shape[0]
    low_acc = jnp.zeros(kernels.shape[:-2] + (col_count,), jnp.float32)
    high_acc = jnp.zeros(kernels.shape[:-2] + (col_count,), jnp.float32)
    for row_off in range(KERNEL):
        for col_off in range(KERNEL):
            window = padded[..., row_off:row_off + row_count, col_off:col_off + col_count]
            tap_at = row_off * KERNEL + col_off
            low_acc = low_acc + kernels[..., 0, tap_at][..., None] * window
            high_acc = high_acc + kernels[..., 1, tap_at][..., None] * window
    return (1.0 - blend_map) * low_acc + blend_map * high_acc


def reference(images, valid_mask, basis_index, match_index, psf_bank):
    rim_width = KERNEL // 2
    width_all = images.shape[2]
    blend_map = jnp.arange(width_all).astype(jnp.float32) / (width_all - 1)
    normed = psf_bank / jnp.sum(psf_bank, axis=1, keepdims=True)

    def warp_one(items):
        source, tile_index = items
        kernels = jnp.repeat(normed[tile_index], TILE_ROWS, axis=0)
        return vary_conv(jnp.pad(source, rim_width), kernels, blend_map)

    warped = lax.map(warp_one, (images, basis_index))
    is_valid = valid_mask == 1
    total_sum = jnp.sum(jnp.where(is_valid, warped, 0.0), axis=0)
    valid_count = jnp.sum(valid_mask, axis=0).astype(jnp.float32)
    low_three = jnp.sort(jnp.where(is_valid, warped, sentinel), axis=0)[:3]
    high_three = jnp.sort(jnp.where(is_valid, warped, -sentinel), axis=0)[-3:]
    low_sum = low_three[0] + low_three[1] + low_three[2]
    high_sum = high_three[2] + high_three[1] + high_three[0]
    coadd_image = (total_sum - low_sum - high_sum) / (valid_count - 6.0)
    coadd_padded = jnp.pad(coadd_image, rim_width)

    def match_one(tile_index):
        kernels = jnp.repeat(normed[tile_index], TILE_ROWS, axis=0)
        return vary_conv(coadd_padded, kernels, blend_map)

    matched = lax.map(match_one, match_index)
    return coadd_image, images - matched
```

```python
import functools

import jax
import jax.numpy as jnp
from jax import lax
from jax.experimental import pallas as pl
from jax.experimental.pallas import tpu as pltpu
from jax.sharding import PartitionSpec as P

TILE_ROWS = 16
KERNEL = 9
RIM = KERNEL // 2
SLOTS = TILE_ROWS + 2 * RIM
LANES = 128
DEPTH = 256
SENTINEL = 1.0e30
LIMIT = 1.0e29

VMEM = pl.BlockSpec(memory_space=pltpu.VMEM)
SMEM = pl.BlockSpec(memory_space=pltpu.SMEM)


def call(body, outs, specs, flops, size):
    single = not isinstance(outs, (list, tuple))
    return pl.pallas_call(
        body,
        out_shape=outs,
        in_specs=specs,
        out_specs=VMEM if single else [VMEM] * len(outs),
        compiler_params=pltpu.CompilerParams(vmem_limit_bytes=12 << 20),
        cost_estimate=pl.CostEstimate(flops=flops, bytes_accessed=size, transcendentals=0),
    )


def iota(shape, dim):
    return lax.broadcasted_iota(jnp.int32, shape, dim)


def split(value):
    high = value.astype(jnp.bfloat16)
    low = (value - high.astype(jnp.float32)).astype(jnp.bfloat16)
    return high, low


def blend_row(col_count):
    columns = lax.axis_index("band") * col_count + iota((1, col_count), 1)
    return columns.astype(jnp.float32) / float(col_count * lax.axis_size("band") - 1)


def tap_body(bank_ref, out_ref):
    bank = bank_ref[...]
    normed = bank / jnp.sum(bank, axis=1, keepdims=True)
    tap = iota((KERNEL * KERNEL, DEPTH), 0)
    row_off = (tap * 57) >> 9
    col_off = tap - row_off * KERNEL
    place = (iota((KERNEL * KERNEL, DEPTH), 1) == col_off * SLOTS + row_off).astype(jnp.float32)
    first = jnp.dot(normed, place, precision=lax.Precision.HIGHEST, preferred_element_type=jnp.float32)
    lane = iota((TILE_ROWS, DEPTH), 1)
    slot = lane - SLOTS * ((lane * 2731) >> 16)
    for base in range(bank.shape[0]):
        spread = jnp.broadcast_to(first[base : base + 1], (TILE_ROWS, DEPTH))
        rows = pltpu.roll(spread, 0, 1, stride=1, stride_axis=0)
        wrapped = jnp.where(slot < SLOTS - RIM, pltpu.roll(rows, DEPTH - RIM, 1), pltpu.roll(rows, SLOTS - RIM, 1))
        high, low = split(wrapped)
        out_ref[base, :TILE_ROWS, :] = high
        out_ref[base, TILE_ROWS:, :] = low


def shifted(rows):
    width = rows.shape[1]
    cols = width - LANES
    parts = []
    for col_off in range(KERNEL):
        amount = (RIM - col_off) % width
        moved = rows if amount == 0 else pltpu.roll(rows, amount, 1)
        parts.append(moved[:, :cols])
    parts.append(jnp.zeros((DEPTH - KERNEL * SLOTS, cols), jnp.float32))
    return split(jnp.concatenate(parts, axis=0))


def edge(first, last, has_first, has_last, lane):
    return jnp.where((lane < RIM) & has_first, first, 0.0) + jnp.where((lane >= LANES - RIM) & has_last, last, 0.0)


def sides():
    strip = lax.axis_index("strip")
    band = lax.axis_index("band")
    return (
        strip > 0,
        strip < lax.axis_size("strip") - 1,
        band > 0,
        band < lax.axis_size("band") - 1,
    )


def pack_body(swap_rows, swap_cols, images_ref, *outs):
    count, rows, cols = images_ref.shape
    above, below, left, right = sides()
    sub = iota((8, cols), 0)
    lane = iota((rows, LANES), 1)
    ups, downs = [], []
    for pair in range(count // 2):
        head = [images_ref[2 * pair + k, 0:8, :] for k in range(2)]
        tail = [images_ref[2 * pair + k, rows - 8 : rows, :] for k in range(2)]
        ups.append(jnp.where(sub < RIM, head[0], pltpu.roll(head[1], RIM, 0)))
        downs.append(jnp.where(sub < RIM, pltpu.roll(tail[0], RIM, 0), tail[1]))
    lefts = jnp.zeros((rows, LANES), jnp.float32)
    rights = jnp.zeros((rows, LANES), jnp.float32)
    for e in range(count):
        here = (lane >= RIM * e) & (lane < RIM * (e + 1))
        lefts = jnp.where(here, pltpu.roll(images_ref[e, :, :LANES], RIM * e, 1) if e else images_ref[e, :, :LANES], lefts)
        rights = jnp.where(here, pltpu.roll(images_ref[e, :, cols - LANES :], (RIM * (e + 1)) % LANES, 1), rights)
    outs = list(outs)
    if swap_rows:
        out = outs.pop(0)
        for pair in range(count // 2):
            out[8 * pair : 8 * pair + 8, :] = jnp.where(below, downs[pair], ups[pair])
    else:
        up, down = outs.pop(0), outs.pop(0)
        for pair in range(count // 2):
            up[8 * pair : 8 * pair + 8, :] = ups[pair]
            down[8 * pair : 8 * pair + 8, :] = downs[pair]
    if swap_cols:
        edges = [jnp.where(right, rights, lefts)]
    else:
        edges = [lefts, rights]
    for value in edges:
        outs.pop(0)[...] = value
    for value in edges:
        if swap_rows:
            outs.pop(0)[...] = jnp.where(below, value[rows - 8 :], value[:8])
        else:
            outs.pop(0)[...] = value[:8]
            outs.pop(0)[...] = value[rows - 8 :]


def warp_body(
    sent, images_ref, mask_ref, index_ref, taps_ref, above_ref, below_ref, left_ref, right_ref, c_al, c_ar, c_bl, c_br, out_ref
):
    count, rows, cols = images_ref.shape
    tiles = rows // TILE_ROWS
    above, below, left, right = sides()
    parity = (lax.axis_index("exp") + lax.axis_index("strip")) % 2
    tile = (1 - parity) if sent else parity
    start = pl.multiple_of(tile * TILE_ROWS, TILE_ROWS)
    prior = pl.multiple_of(jnp.maximum(start - 8, 0), 8)
    after = pl.multiple_of(jnp.minimum(start + TILE_ROWS, rows - 8), 8)
    top = tile == 0
    end = tile == tiles - 1
    sub = iota((8, cols), 0)
    sub_l = iota((8, LANES), 0)
    lane_l = iota((8, LANES), 1)
    lane_m = iota((TILE_ROWS, LANES), 1)
    blend = blend_row(cols)

    def put(first, last, e, lane):
        first = pltpu.roll(first, (LANES - RIM * e) % LANES, 1) if e else first
        last = pltpu.roll(last, (LANES - RIM - RIM * e) % LANES, 1)
        return edge(first, last, right, left, lane)

    rim_first = jnp.where(
        sub_l < RIM,
        jnp.where(end, jnp.where(below, c_br[...], 0.0), right_ref[pl.ds(after, 8), :]),
        jnp.where(top, jnp.where(above, c_ar[...], 0.0), right_ref[pl.ds(prior, 8), :]),
    )
    rim_last = jnp.where(
        sub_l < RIM,
        jnp.where(end, jnp.where(below, c_bl[...], 0.0), left_ref[pl.ds(after, 8), :]),
        jnp.where(top, jnp.where(above, c_al[...], 0.0), left_ref[pl.ds(prior, 8), :]),
    )
    main_first = right_ref[pl.ds(start, TILE_ROWS), :]
    main_last = left_ref[pl.ds(start, TILE_ROWS), :]
    for e in range(count):
        group = 8 * (e // 2)
        low_rows = below_ref[group : group + 8, :]
        high_rows = above_ref[group : group + 8, :]
        if e % 2:
            low_rows = pltpu.roll(low_rows, RIM, 0)
        else:
            high_rows = pltpu.roll(high_rows, RIM, 0)
        rim = jnp.where(
            sub < RIM,
            jnp.where(end, jnp.where(below, low_rows, 0.0), images_ref[e, pl.ds(after, 8), :]),
            jnp.where(top, jnp.where(above, high_rows, 0.0), images_ref[e, pl.ds(prior, 8), :]),
        )
        body = jnp.concatenate([images_ref[e, pl.ds(start, TILE_ROWS), :], rim], axis=0)
        edges = jnp.concatenate([put(main_first, main_last, e, lane_m), put(rim_first, rim_last, e, lane_l)], axis=0)
        high, low = shifted(jnp.concatenate([body, edges], axis=1))
        taps = jnp.concatenate([taps_ref[index_ref[e, tile, 0]], taps_ref[index_ref[e, tile, 1]]], axis=0)
        sums = jnp.dot(taps, high, preferred_element_type=jnp.float32) + jnp.dot(taps, low, preferred_element_type=jnp.float32)
        n = TILE_ROWS
        first = sums[0:n] + sums[n : 2 * n]
        second = sums[2 * n : 3 * n] + sums[3 * n : 4 * n]
        warped = (1.0 - blend) * first + blend * second
        out_ref[e] = jnp.where(mask_ref[e, pl.ds(start, TILE_ROWS), :] == 1, warped, SENTINEL)


def insert_low(three, value):
    a, b, c = three
    over = jnp.maximum(a, value)
    a = jnp.minimum(a, value)
    more = jnp.maximum(b, over)
    b = jnp.minimum(b, over)
    return a, b, jnp.minimum(c, more)


def insert_high(three, value):
    a, b, c = three
    under = jnp.minimum(a, value)
    a = jnp.maximum(a, value)
    less = jnp.minimum(b, under)
    b = jnp.maximum(b, under)
    return a, b, jnp.maximum(c, less)


def gather_body(own_ref, other_ref, out_ref):
    count, rows, cols = own_ref.shape
    big = jnp.full((8, LANES), SENTINEL, jnp.float32)
    for r in range(0, rows, 8):
        for c in range(0, cols, LANES):
            total = jnp.zeros((8, LANES), jnp.float32)
            number = jnp.zeros((8, LANES), jnp.float32)
            low, high = (big, big, big), (-big, -big, -big)
            for ref in (own_ref, other_ref):
                for e in range(count):
                    value = ref[e, r : r + 8, c : c + LANES]
                    valid = value < LIMIT
                    total = total + jnp.where(valid, value, 0.0)
                    number = number + jnp.where(valid, 1.0, 0.0)
                    low = insert_low(low, value)
                    high = insert_high(high, jnp.where(valid, value, -SENTINEL))
            for k, plane in enumerate((total, number) + low + high):
                out_ref[k, r : r + 8, c : c + LANES] = plane


def merge_low(a, b):
    return (
        jnp.minimum(a[0], b[0]),
        jnp.minimum(jnp.minimum(a[1], b[1]), jnp.maximum(a[0], b[0])),
        jnp.minimum(jnp.minimum(a[2], b[2]), jnp.minimum(jnp.maximum(a[1], b[0]), jnp.maximum(a[0], b[1]))),
    )


def merge_high(a, b):
    return (
        jnp.maximum(a[0], b[0]),
        jnp.maximum(jnp.maximum(a[1], b[1]), jnp.minimum(a[0], b[0])),
        jnp.maximum(jnp.maximum(a[2], b[2]), jnp.maximum(jnp.minimum(a[1], b[0]), jnp.minimum(a[0], b[1]))),
    )


def merge_body(last, own_ref, other_ref, out_ref):
    _, rows, cols = own_ref.shape
    for r in range(0, rows, 8):
        for c in range(0, cols, LANES):
            a = [own_ref[k, r : r + 8, c : c + LANES] for k in range(8)]
            b = [other_ref[k, r : r + 8, c : c + LANES] for k in range(8)]
            total, number = a[0] + b[0], a[1] + b[1]
            low = merge_low(a[2:5], b[2:5])
            high = merge_high(a[5:8], b[5:8])
            if last:
                low_sum = low[0] + low[1] + low[2]
                high_sum = high[0] + high[1] + high[2]
                out_ref[r : r + 8, c : c + LANES] = (total - low_sum - high_sum) / (number - 6.0)
            else:
                for k, plane in enumerate((total, number) + low + high):
                    out_ref[k, r : r + 8, c : c + LANES] = plane


def join_body(swap_cols, own_ref, pair_ref, a_same, a_cross, b_same, b_cross, coadd_ref, rim_ref, *outs):
    above, below, left, right = sides()
    parity = (lax.axis_index("exp") + lax.axis_index("strip")) % 2
    even = parity == 0
    own, pair = own_ref[...], pair_ref[...]
    n, cols = own.shape
    coadd_ref[:n, :] = jnp.where(even, own, pair)
    coadd_ref[n:, :] = jnp.where(even, pair, own)
    sub = iota((8, cols), 0)
    low = jnp.where(even, b_cross[:8, :], b_same[:8, :])
    high = jnp.where(even, a_same[n - 8 :, :], a_cross[n - 8 :, :])
    rim_ref[...] = jnp.where(sub < RIM, jnp.where(below, low, 0.0), jnp.where(above, high, 0.0))
    for ref, at in ((coadd_ref, 0), (rim_ref, 2 * n)):
        rows = ref.shape[0]
        lefts, rights = ref[:, :LANES], ref[:, cols - LANES :]
        if swap_cols:
            outs[0][at : at + rows, :] = jnp.where(right, rights, lefts)
        else:
            outs[0][at : at + rows, :] = lefts
            outs[1][at : at + rows, :] = rights


def match_body(images_ref, index_ref, taps_ref, coadd_ref, rim_ref, left_ref, right_ref, out_ref):
    count, rows, cols = images_ref.shape
    tiles = rows // TILE_ROWS
    _, _, left, right = sides()
    blend = blend_row(cols)
    sub = iota((8, cols), 0)
    lane = iota((rows + 8, LANES), 1)
    sub_l = iota((8, LANES), 0)
    edges = edge(right_ref[...], left_ref[...], right, left, lane)
    n = TILE_ROWS
    for tile in range(tiles):
        start = tile * n

        def rims(main, last, at):
            low = last if tile == tiles - 1 else main[start + n : start + n + 8]
            high = last if tile == 0 else main[start - 8 : start]
            return jnp.concatenate([main[start : start + n], jnp.where(at < RIM, low, high)], axis=0)

        body = rims(coadd_ref[...], rim_ref[...], sub)
        side = rims(edges[:rows], edges[rows:], sub_l)
        high, low = shifted(jnp.concatenate([body, side], axis=1))
        taps = jnp.concatenate([taps_ref[index_ref[e, tile, k]] for e in range(count) for k in range(2)], axis=0)
        sums = jnp.dot(taps, high, preferred_element_type=jnp.float32) + jnp.dot(taps, low, preferred_element_type=jnp.float32)
        for e in range(count):
            at = 4 * n * e
            first = sums[at : at + n] + sums[at + n : at + 2 * n]
            second = sums[at + 2 * n : at + 3 * n] + sums[at + 3 * n : at + 4 * n]
            out_ref[e, start : start + n, :] = images_ref[e, start : start + n, :] - (
                (1.0 - blend) * first + blend * second
            )


def moved(value, exp_bit, strip_step, band_step):
    sizes = [lax.axis_size(a) for a in ("exp", "strip", "band")]
    pairs = []
    for z in range(sizes[0]):
        for s in range(sizes[1]):
            for b in range(sizes[2]):
                s_from, b_from = s + strip_step, b + band_step
                if sizes[1] == 2:
                    s_from %= 2
                if sizes[2] == 2:
                    b_from %= 2
                if 0 <= s_from < sizes[1] and 0 <= b_from < sizes[2]:
                    source = ((z ^ exp_bit) * sizes[1] + s_from) * sizes[2] + b_from
                    pairs.append((source, (z * sizes[1] + s) * sizes[2] + b))
    return lax.ppermute(value, ("exp", "strip", "band"), pairs)


def on_device(images, valid_mask, basis_index, match_index, psf_bank):
    count, rows, cols = images.shape
    strips, bands, layers = lax.axis_size("strip"), lax.axis_size("band"), lax.axis_size("exp")
    swap_rows, swap_cols = strips == 2, bands == 2
    f32 = lambda *shape: jax.ShapeDtypeStruct(shape, jnp.float32)
    area = rows * cols

    row_outs = [f32(RIM * count, cols)] * (1 if swap_rows else 2)
    col_outs = [f32(rows, LANES)] * (1 if swap_cols else 2)
    corner_outs = [f32(8, LANES)] * (len(row_outs) * len(col_outs))
    packed = call(
        functools.partial(pack_body, swap_rows, swap_cols), row_outs + col_outs + corner_outs, [VMEM], 100000, 300000
    )(images)
    packed = list(packed)
    ups = [packed.pop(0) for _ in row_outs]
    edges = [packed.pop(0) for _ in col_outs]
    if swap_rows:
        above = below = moved(ups[0], 0, 1, 0)
    else:
        below, above = moved(ups[0], 0, 1, 0), moved(ups[1], 0, -1, 0)
    if swap_cols:
        left = right = moved(edges[0], 0, 0, 1)
    else:
        right, left = moved(edges[0], 0, 0, 1), moved(edges[1], 0, 0, -1)
    corners = {}
    for c in range(len(col_outs)):
        for r in range(len(row_outs)):
            value = packed.pop(0)
            corners[(r, c)] = moved(value, 0, 1 if r == 0 else -1, 1 if c == 0 else -1)
    at = lambda r, c: corners[(0 if swap_rows else r, 0 if swap_cols else c)]
    rims = (above, below, left, right, at(1, 1), at(1, 0), at(0, 1), at(0, 0))

    banks = psf_bank.shape[0]
    taps = call(tap_body, jax.ShapeDtypeStruct((banks, 2 * TILE_ROWS, DEPTH), jnp.bfloat16), [VMEM], 10000000, 300000)(psf_bank)

    def warp(sent):
        return call(
            functools.partial(warp_body, sent),
            f32(count, TILE_ROWS, cols),
            [VMEM, VMEM, SMEM, VMEM] + [VMEM] * 8,
            4 * TILE_ROWS * DEPTH * cols * count * 4,
            1000000,
        )(images, valid_mask, basis_index, taps, *rims)

    sent = moved(warp(True), 1, 0, 0)
    state = call(gather_body, f32(8, TILE_ROWS, cols), [VMEM, VMEM], area * 100, 400000)(warp(False), sent)
    bit = 2
    while bit < layers:
        last = 2 * bit == layers
        out = f32(TILE_ROWS, cols) if last else f32(8, TILE_ROWS, cols)
        state = call(functools.partial(merge_body, last), out, [VMEM, VMEM], area * 20, 300000)(
            state, moved(state, bit, 0, 0)
        )
        bit *= 2
    pair = moved(state, 1, 0, 0)
    if swap_rows:
        same = moved(state, 0, 1, 0)
        cross = moved(state, 1, 1, 0)
        near = (same, cross, same, cross)
    else:
        near = (moved(state, 0, -1, 0), moved(state, 1, -1, 0), moved(state, 0, 1, 0), moved(state, 1, 1, 0))
    side_outs = [f32(rows + 8, LANES)] * (1 if swap_cols else 2)
    coadd, rim, *side = call(
        functools.partial(join_body, swap_cols), [f32(rows, cols), f32(8, cols)] + side_outs, [VMEM] * 6, 10000, 100000
    )(state, pair, *near)
    if swap_cols:
        left = right = moved(side[0], 0, 0, 1)
    else:
        right, left = moved(side[0], 0, 0, 1), moved(side[1], 0, 0, -1)
    difference = call(
        match_body, f32(count, rows, cols), [VMEM, SMEM, VMEM] + [VMEM] * 4, 8 * area * DEPTH * count, 1000000
    )(images, match_index, taps, coadd, rim, left, right)
    return coadd, difference


def solution(mesh):
    return jax.shard_map(
        on_device,
        mesh=mesh,
        in_specs=(
            P(("patch", "exp"), "strip", "band"),
            P(("patch", "exp"), "strip", "band"),
            P(("patch", "exp"), "strip", None),
            P(("patch", "exp"), "strip", None),
            P(),
        ),
        out_specs=(P(("patch", "strip"), "band"), P(("patch", "exp"), "strip", "band")),
        check_vma=False,
    )
```

```python
import functools

import jax
import jax.numpy as jnp
from jax import lax
from jax.experimental import pallas as pl
from jax.experimental.pallas import tpu as pltpu
from jax.sharding import PartitionSpec as P

TILE_ROWS = 16
KERNEL = 9
GROUP = 3
RIM = KERNEL // 2
SLOTS = TILE_ROWS + 2 * RIM
LANES = 128
DEPTH = 256
SENTINEL = 1.0e30
LIMIT = 1.0e29
CHUNKS = 2

VMEM = pl.BlockSpec(memory_space=pltpu.VMEM)
SMEM = pl.BlockSpec(memory_space=pltpu.SMEM)


def call(body, outs, specs, flops, size, scratch=()):
    single = not isinstance(outs, (list, tuple))
    return pl.pallas_call(
        body,
        out_shape=outs,
        in_specs=specs,
        out_specs=VMEM if single else [VMEM] * len(outs),
        scratch_shapes=scratch,
        compiler_params=pltpu.CompilerParams(vmem_limit_bytes=12 << 20),
        cost_estimate=pl.CostEstimate(flops=flops, bytes_accessed=size, transcendentals=0),
    )


def iota(shape, dim):
    return lax.broadcasted_iota(jnp.int32, shape, dim)


def split(value):
    high = value.astype(jnp.bfloat16)
    low = (value - high.astype(jnp.float32)).astype(jnp.bfloat16)
    return high, low


def blend_row(col_count):
    columns = lax.axis_index("band") * col_count + iota((1, col_count), 1)
    return columns.astype(jnp.float32) / float(col_count * lax.axis_size("band") - 1)


def tap_rows(bank_ref):
    bank = bank_ref[...]
    normed = bank / jnp.sum(bank, axis=1, keepdims=True)
    tap = iota((KERNEL * KERNEL, DEPTH), 0)
    row_off = (tap * 57) >> 9
    col_off = tap - row_off * KERNEL
    place = (iota((KERNEL * KERNEL, DEPTH), 1) == col_off * SLOTS + row_off).astype(jnp.float32)
    first = jnp.dot(normed, place, precision=lax.Precision.HIGHEST, preferred_element_type=jnp.float32)
    lane = iota((TILE_ROWS, DEPTH), 1)
    slot = lane - SLOTS * ((lane * 2731) >> 16)
    for base in range(bank.shape[0]):
        spread = jnp.broadcast_to(first[base : base + 1], (TILE_ROWS, DEPTH))
        rows = pltpu.roll(spread, 0, 1, stride=1, stride_axis=0)
        yield base, jnp.where(slot < SLOTS - RIM, pltpu.roll(rows, DEPTH - RIM, 1), pltpu.roll(rows, SLOTS - RIM, 1))


def match_taps_body(bank_ref, index_ref, _, out_ref, all_ref):
    tiles, pair, count = index_ref.shape
    n = 2 * TILE_ROWS
    for base, rows in tap_rows(bank_ref):
        high, low = split(rows)
        all_ref[base, :TILE_ROWS, :] = high
        all_ref[base, TILE_ROWS:, :] = low
    for tile in range(tiles):
        for e in range(count):
            for k in range(pair):
                at = n * (2 * e + k)
                out_ref[tile, at : at + n, :] = all_ref[index_ref[tile, k, e]]


def warp_taps_body(bank_ref, index_ref, out_ref, all_ref):
    tiles, pair, count = index_ref.shape
    lane = iota((TILE_ROWS, DEPTH), 1)
    part = GROUP * SLOTS
    n = GROUP * TILE_ROWS
    for base, rows in tap_rows(bank_ref):
        high = rows.astype(jnp.bfloat16).astype(jnp.float32)
        low = rows - high
        turned = {(0, 0): high, (1, 0): low}

        def turn(which, steps):
            if (which, steps) not in turned:
                turned[which, steps] = pltpu.roll((high, low)[which], (part * steps) % DEPTH, 1)
            return turned[which, steps]

        for g in range(GROUP):
            value = jnp.where(lane < part, turn(0, -g), jnp.where(lane < 2 * part, turn(0, 1 - g), turn(1, 2 - g)))
            value = jnp.where(lane < 3 * part, value, 0.0)
            all_ref[base, g * TILE_ROWS : (g + 1) * TILE_ROWS, :] = value.astype(jnp.bfloat16)
    for tile in range(tiles):
        for e in range(count):
            for k in range(pair):
                out_ref[tile, e, k * n : (k + 1) * n, :] = all_ref[index_ref[tile, k, e]]


def shifted(rows):
    width = rows.shape[1]
    cols = width - LANES
    parts = []
    for col_off in range(KERNEL):
        amount = (RIM - col_off) % width
        moved = rows if amount == 0 else pltpu.roll(rows, amount, 1)
        parts.append(moved[:, :cols])
    parts.append(jnp.zeros((DEPTH - KERNEL * SLOTS, cols), jnp.float32))
    return split(jnp.concatenate(parts, axis=0))


def edge(first, last, has_first, has_last, lane):
    return jnp.where((lane < RIM) & has_first, first, 0.0) + jnp.where((lane >= LANES - RIM) & has_last, last, 0.0)


def sides():
    strip = lax.axis_index("strip")
    band = lax.axis_index("band")
    return (
        strip > 0,
        strip < lax.axis_size("strip") - 1,
        band > 0,
        band < lax.axis_size("band") - 1,
    )


def pack_body(swap_rows, swap_cols, images_ref, *outs):
    count, rows, cols = images_ref.shape
    above, below, left, right = sides()
    sub = iota((8, cols), 0)
    lane = iota((rows, LANES), 1)
    ups, downs = [], []
    for pair in range(count // 2):
        head = [images_ref[2 * pair + k, 0:8, :] for k in range(2)]
        tail = [images_ref[2 * pair + k, rows - 8 : rows, :] for k in range(2)]
        ups.append(jnp.where(sub < RIM, head[0], pltpu.roll(head[1], RIM, 0)))
        downs.append(jnp.where(sub < RIM, pltpu.roll(tail[0], RIM, 0), tail[1]))
    lefts = jnp.zeros((rows, LANES), jnp.float32)
    rights = jnp.zeros((rows, LANES), jnp.float32)
    for e in range(count):
        here = (lane >= RIM * e) & (lane < RIM * (e + 1))
        lefts = jnp.where(here, pltpu.roll(images_ref[e, :, :LANES], RIM * e, 1) if e else images_ref[e, :, :LANES], lefts)
        rights = jnp.where(here, pltpu.roll(images_ref[e, :, cols - LANES :], (RIM * (e + 1)) % LANES, 1), rights)
    outs = list(outs)
    if swap_rows:
        out = outs.pop(0)
        for pair in range(count // 2):
            out[8 * pair : 8 * pair + 8, :] = jnp.where(below, downs[pair], ups[pair])
    else:
        up, down = outs.pop(0), outs.pop(0)
        for pair in range(count // 2):
            up[8 * pair : 8 * pair + 8, :] = ups[pair]
            down[8 * pair : 8 * pair + 8, :] = downs[pair]
    if swap_cols:
        edges = [jnp.where(right, rights, lefts)]
    else:
        edges = [lefts, rights]
    for value in edges:
        outs.pop(0)[...] = value
    for value in edges:
        if swap_rows:
            outs.pop(0)[...] = jnp.where(below, value[rows - 8 :], value[:8])
        else:
            outs.pop(0)[...] = value[:8]
            outs.pop(0)[...] = value[rows - 8 :]


def warp_body(
    sent, blocks, images_ref, mask_ref, taps_ref, above_ref, below_ref, left_ref, right_ref, c_al, c_ar, c_bl, c_br, out_ref
):
    count, rows, cols = images_ref.shape
    tiles = rows // TILE_ROWS
    above, below, left, right = sides()
    parity = (lax.axis_index("exp") + lax.axis_index("strip")) % 2
    tile = (1 - parity) if sent else parity
    start = pl.multiple_of(tile * TILE_ROWS, TILE_ROWS)
    prior = pl.multiple_of(jnp.maximum(start - 8, 0), 8)
    after = pl.multiple_of(jnp.minimum(start + TILE_ROWS, rows - 8), 8)
    top = tile == 0
    end = tile == tiles - 1
    sub = iota((8, LANES), 0)
    lane = iota((SLOTS, LANES), 1)
    blend = blend_row(cols)
    width = 2 * LANES

    def side(ref, corner_above, corner_below):
        rim = jnp.where(
            sub < RIM,
            jnp.where(end, jnp.where(below, corner_below[...], 0.0), ref[pl.ds(after, 8), :]),
            jnp.where(top, jnp.where(above, corner_above[...], 0.0), ref[pl.ds(prior, 8), :]),
        )
        return jnp.concatenate([ref[pl.ds(start, TILE_ROWS), :], rim], axis=0)

    rights = jnp.where(right, side(right_ref, c_ar, c_br), 0.0)
    lefts = jnp.where(left, side(left_ref, c_al, c_bl), 0.0)
    last = cols // LANES - 1

    def source(e, block):
        if block < 0:
            return pltpu.roll(lefts, (LANES - RIM - RIM * e) % LANES, 1)
        if block > last:
            return pltpu.roll(rights, (LANES - RIM * e) % LANES, 1) if e else rights
        at = slice(block * LANES, (block + 1) * LANES)
        group = slice(8 * (e // 2), 8 * (e // 2) + 8)
        low_rows, high_rows = below_ref[group, at], above_ref[group, at]
        if e % 2:
            low_rows = pltpu.roll(low_rows, RIM, 0)
        else:
            high_rows = pltpu.roll(high_rows, RIM, 0)
        rim = jnp.where(
            sub < RIM,
            jnp.where(end, jnp.where(below, low_rows, 0.0), images_ref[e, pl.ds(after, 8), at]),
            jnp.where(top, jnp.where(above, high_rows, 0.0), images_ref[e, pl.ds(prior, 8), at]),
        )
        return jnp.concatenate([images_ref[e, pl.ds(start, TILE_ROWS), at], rim], axis=0)

    zero = jnp.zeros((DEPTH - 3 * GROUP * SLOTS, width), jnp.float32)
    for e in range(count):
        taps = taps_ref[tile, e]
        seen = {}

        def get(block):
            if block not in seen:
                seen[block] = source(e, block)
            return seen[block]

        for order, block in enumerate(blocks):
            rim = jnp.where(lane < RIM, get(block + 1), get(block - 1))
            field = jnp.concatenate([get(block), rim], axis=1)
            near = jnp.concatenate([pltpu.roll(field, 1, 1), field, pltpu.roll(field, width - 1, 1)], axis=0)
            high = near.astype(jnp.bfloat16).astype(jnp.float32)
            stack = jnp.concatenate([high, near - high, high, zero], axis=0).astype(jnp.bfloat16)
            sums = jnp.dot(taps, stack, preferred_element_type=jnp.float32)
            n = TILE_ROWS
            pair = []
            for k in range(2):
                at = k * GROUP * n
                pair.append(
                    pltpu.roll(sums[at : at + n], GROUP, 1)[:, :LANES]
                    + sums[at + n : at + 2 * n, :LANES]
                    + pltpu.roll(sums[at + 2 * n : at + 3 * n], width - GROUP, 1)[:, :LANES]
                )
            here = blend[:, block * LANES : (block + 1) * LANES]
            warped = (1.0 - here) * pair[0] + here * pair[1]
            valid = mask_ref[e, pl.ds(start, TILE_ROWS), block * LANES : (block + 1) * LANES] == 1
            out_ref[e, :, order * LANES : (order + 1) * LANES] = jnp.where(valid, warped, SENTINEL)


def insert_low(three, value):
    a, b, c = three
    over = jnp.maximum(a, value)
    a = jnp.minimum(a, value)
    more = jnp.maximum(b, over)
    b = jnp.minimum(b, over)
    return a, b, jnp.minimum(c, more)


def insert_high(three, value):
    a, b, c = three
    under = jnp.minimum(a, value)
    a = jnp.maximum(a, value)
    less = jnp.minimum(b, under)
    b = jnp.maximum(b, under)
    return a, b, jnp.maximum(c, less)


def gather_body(first, own_ref, other_ref, out_ref):
    count, rows, cols = other_ref.shape
    big = jnp.full((8, LANES), SENTINEL, jnp.float32)
    for r in range(0, rows, 8):
        for c in range(0, cols, LANES):
            total = jnp.zeros((8, LANES), jnp.float32)
            number = jnp.zeros((8, LANES), jnp.float32)
            low, high = (big, big, big), (-big, -big, -big)
            for ref, at in ((own_ref, c + first), (other_ref, c)):
                for e in range(count):
                    value = ref[e, r : r + 8, at : at + LANES]
                    valid = value < LIMIT
                    total = total + jnp.where(valid, value, 0.0)
                    number = number + jnp.where(valid, 1.0, 0.0)
                    low = insert_low(low, value)
                    high = insert_high(high, jnp.where(valid, value, -SENTINEL))
            for k, plane in enumerate((total, number) + low + high):
                out_ref[k, r : r + 8, c : c + LANES] = plane


def merge_low(a, b):
    return (
        jnp.minimum(a[0], b[0]),
        jnp.minimum(jnp.minimum(a[1], b[1]), jnp.maximum(a[0], b[0])),
        jnp.minimum(jnp.minimum(a[2], b[2]), jnp.minimum(jnp.maximum(a[1], b[0]), jnp.maximum(a[0], b[1]))),
    )


def merge_high(a, b):
    return (
        jnp.maximum(a[0], b[0]),
        jnp.maximum(jnp.maximum(a[1], b[1]), jnp.minimum(a[0], b[0])),
        jnp.maximum(jnp.maximum(a[2], b[2]), jnp.maximum(jnp.minimum(a[1], b[0]), jnp.minimum(a[0], b[1]))),
    )


def merge_body(last, _, *refs):
    *inputs, out_ref = refs
    for piece in range(len(inputs) // 2):
        own_ref, other_ref = inputs[2 * piece : 2 * piece + 2]
        _, rows, cols = own_ref.shape
        for r in range(0, rows, 8):
            for c in range(0, cols, LANES):
                a = [own_ref[k, r : r + 8, c : c + LANES] for k in range(8)]
                b = [other_ref[k, r : r + 8, c : c + LANES] for k in range(8)]
                total, number = a[0] + b[0], a[1] + b[1]
                low = merge_low(a[2:5], b[2:5])
                high = merge_high(a[5:8], b[5:8])
                at = piece * cols + c
                if last:
                    low_sum = low[0] + low[1] + low[2]
                    high_sum = high[0] + high[1] + high[2]
                    out_ref[r : r + 8, at : at + LANES] = (total - low_sum - high_sum) / (number - 6.0)
                else:
                    for k, plane in enumerate((total, number) + low + high):
                        out_ref[k, r : r + 8, at : at + LANES] = plane


def join_body(swap_cols, own_ref, pair_ref, a_same, a_cross, b_same, b_cross, coadd_ref, rim_ref, *outs):
    above, below, left, right = sides()
    parity = (lax.axis_index("exp") + lax.axis_index("strip")) % 2
    even = parity == 0
    own, pair = own_ref[...], pair_ref[...]
    n, cols = own.shape
    coadd_ref[:n, :] = jnp.where(even, own, pair)
    coadd_ref[n:, :] = jnp.where(even, pair, own)
    sub = iota((8, cols), 0)
    low = jnp.where(even, b_cross[:8, :], b_same[:8, :])
    high = jnp.where(even, a_same[n - 8 :, :], a_cross[n - 8 :, :])
    rim_ref[...] = jnp.where(sub < RIM, jnp.where(below, low, 0.0), jnp.where(above, high, 0.0))
    for ref, at in ((coadd_ref, 0), (rim_ref, 2 * n)):
        rows = ref.shape[0]
        lefts, rights = ref[:, :LANES], ref[:, cols - LANES :]
        if swap_cols:
            outs[0][at : at + rows, :] = jnp.where(right, rights, lefts)
        else:
            outs[0][at : at + rows, :] = lefts
            outs[1][at : at + rows, :] = rights


def match_body(images_ref, taps_ref, coadd_ref, rim_ref, left_ref, right_ref, coadd_out, out, out_ref, sems):
    count, rows, cols = images_ref.shape
    tiles = rows // TILE_ROWS
    whole = pltpu.make_async_copy(coadd_ref, coadd_out, sems.at[tiles])
    whole.start()
    _, _, left, right = sides()
    blend = blend_row(cols)
    sub = iota((8, cols), 0)
    lane = iota((rows + 8, LANES), 1)
    sub_l = iota((8, LANES), 0)
    edges = edge(right_ref[...], left_ref[...], right, left, lane)
    n = TILE_ROWS
    copies = []
    for tile in range(tiles):
        start = tile * n

        def rims(main, last, at):
            low = last if tile == tiles - 1 else main[start + n : start + n + 8]
            high = last if tile == 0 else main[start - 8 : start]
            return jnp.concatenate([main[start : start + n], jnp.where(at < RIM, low, high)], axis=0)

        body = rims(coadd_ref[...], rim_ref[...], sub)
        side = rims(edges[:rows], edges[rows:], sub_l)
        high, low = shifted(jnp.concatenate([body, side], axis=1))
        taps = taps_ref[tile]
        sums = jnp.dot(taps, high, preferred_element_type=jnp.float32) + jnp.dot(taps, low, preferred_element_type=jnp.float32)
        for e in range(count):
            at = 4 * n * e
            first = sums[at : at + n] + sums[at + n : at + 2 * n]
            second = sums[at + 2 * n : at + 3 * n] + sums[at + 3 * n : at + 4 * n]
            out_ref[tile, e] = images_ref[e, start : start + n, :] - ((1.0 - blend) * first + blend * second)
        copies.append(pltpu.make_async_copy(out_ref.at[tile], out.at[:, pl.ds(start, n), :], sems.at[tile]))
        copies[-1].start()
    for copy in copies:
        copy.wait()
    whole.wait()


def moved(value, exp_bit, strip_step, band_step):
    sizes = [lax.axis_size(a) for a in ("exp", "strip", "band")]
    pairs = []
    for z in range(sizes[0]):
        for s in range(sizes[1]):
            for b in range(sizes[2]):
                s_from, b_from = s + strip_step, b + band_step
                if sizes[1] == 2:
                    s_from %= 2
                if sizes[2] == 2:
                    b_from %= 2
                if 0 <= s_from < sizes[1] and 0 <= b_from < sizes[2]:
                    source = ((z ^ exp_bit) * sizes[1] + s_from) * sizes[2] + b_from
                    pairs.append((source, (z * sizes[1] + s) * sizes[2] + b))
    return lax.ppermute(value, ("exp", "strip", "band"), pairs)


def on_device(images, valid_mask, basis_index, match_index, psf_bank):
    count, rows, cols = images.shape
    strips, bands, layers = lax.axis_size("strip"), lax.axis_size("band"), lax.axis_size("exp")
    swap_rows, swap_cols = strips == 2, bands == 2
    f32 = lambda *shape: jax.ShapeDtypeStruct(shape, jnp.float32)
    area = rows * cols

    row_outs = [f32(RIM * count, cols)] * (1 if swap_rows else 2)
    col_outs = [f32(rows, LANES)] * (1 if swap_cols else 2)
    corner_outs = [f32(8, LANES)] * (len(row_outs) * len(col_outs))
    packed = call(
        functools.partial(pack_body, swap_rows, swap_cols), row_outs + col_outs + corner_outs, [VMEM], 100000, 300000
    )(images)
    packed = list(packed)
    ups = [packed.pop(0) for _ in row_outs]
    edges = [packed.pop(0) for _ in col_outs]
    if swap_rows:
        above = below = moved(ups[0], 0, 1, 0)
    else:
        below, above = moved(ups[0], 0, 1, 0), moved(ups[1], 0, -1, 0)
    if swap_cols:
        left = right = moved(edges[0], 0, 0, 1)
    else:
        right, left = moved(edges[0], 0, 0, 1), moved(edges[1], 0, 0, -1)
    corners = {}
    for c in range(len(col_outs)):
        for r in range(len(row_outs)):
            value = packed.pop(0)
            corners[(r, c)] = moved(value, 0, 1 if r == 0 else -1, 1 if c == 0 else -1)
    at = lambda r, c: corners[(0 if swap_rows else r, 0 if swap_cols else c)]
    rims = (above, below, left, right, at(1, 1), at(1, 0), at(0, 1), at(0, 0))

    banks = psf_bank.shape[0]
    tiles = rows // TILE_ROWS
    turned = lambda index: jnp.transpose(index, (1, 2, 0))
    scratch = lambda n: [pltpu.VMEM((banks, n, DEPTH), jnp.bfloat16)]
    half = jnp.bfloat16
    warp_taps = call(
        warp_taps_body,
        jax.ShapeDtypeStruct((tiles, count, 2 * GROUP * TILE_ROWS, DEPTH), half),
        [VMEM, SMEM],
        10000000,
        300000,
        scratch(GROUP * TILE_ROWS),
    )(psf_bank, turned(basis_index))

    blocks = list(range(cols // LANES))
    pieces = [blocks] if CHUNKS == 1 else [[b] for b in blocks]

    def warp(sent, piece):
        return call(
            functools.partial(warp_body, sent, piece),
            f32(count, TILE_ROWS, LANES * len(piece)),
            [VMEM, VMEM, VMEM] + [VMEM] * 8,
            2 * TILE_ROWS * DEPTH * LANES * len(piece) * count * 12,
            1000000,
        )(images, valid_mask, warp_taps, *rims)

    sents = [moved(warp(True, piece), 1, 0, 0) for piece in pieces]
    own = warp(False, blocks)
    states = [
        call(functools.partial(gather_body, LANES * piece[0]), f32(8, *sent.shape[1:]), [VMEM, VMEM], area * 100, 400000)(
            own, sent
        )
        for piece, sent in zip(pieces, sents)
    ]
    match_taps = call(
        match_taps_body,
        jax.ShapeDtypeStruct((tiles, 4 * TILE_ROWS * count, DEPTH), half),
        [VMEM, SMEM, pl.BlockSpec(memory_space=pl.ANY)],
        10000000,
        300000,
        scratch(2 * TILE_ROWS),
    )(psf_bank, turned(match_index), states[0])
    bit = 2
    while bit < layers:
        others = [moved(state, bit, 0, 0) for state in states]
        if 2 * bit == layers:
            groups = [[x for both in zip(states, others) for x in both]]
            outs = [f32(TILE_ROWS, cols)]
        else:
            groups = [list(both) for both in zip(states, others)]
            outs = [f32(*state.shape) for state in states]
        states = [
            call(functools.partial(merge_body, 2 * bit == layers), out, [pl.BlockSpec(memory_space=pl.ANY)] + [VMEM] * len(group), area * 20, 300000)(match_taps, *group)
            for out, group in zip(outs, groups)
        ]
        bit *= 2
    (state,) = states
    pair = moved(state, 1, 0, 0)
    if swap_rows:
        same = moved(state, 0, 1, 0)
        cross = moved(state, 1, 1, 0)
        near = (same, cross, same, cross)
    else:
        near = (moved(state, 0, -1, 0), moved(state, 1, -1, 0), moved(state, 0, 1, 0), moved(state, 1, 1, 0))
    side_outs = [f32(rows + 8, LANES)] * (1 if swap_cols else 2)
    coadd, rim, *side = call(
        functools.partial(join_body, swap_cols), [f32(rows, cols), f32(8, cols)] + side_outs, [VMEM] * 6, 10000, 100000
    )(state, pair, *near)
    if swap_cols:
        left = right = moved(side[0], 0, 0, 1)
    else:
        right, left = moved(side[0], 0, 0, 1), moved(side[1], 0, 0, -1)
    return pl.pallas_call(
        match_body,
        out_shape=[f32(rows, cols), f32(count, rows, cols)],
        in_specs=[VMEM] * 6,
        out_specs=[pl.BlockSpec(memory_space=pl.ANY)] * 2,
        scratch_shapes=[pltpu.VMEM((tiles, count, TILE_ROWS, cols), jnp.float32), pltpu.SemaphoreType.DMA((tiles + 1,))],
        compiler_params=pltpu.CompilerParams(vmem_limit_bytes=12 << 20),
        cost_estimate=pl.CostEstimate(flops=8 * area * DEPTH * count, bytes_accessed=1000000, transcendentals=0),
    )(images, match_taps, coadd, rim, left, right)


def solution(mesh):
    return jax.shard_map(
        on_device,
        mesh=mesh,
        in_specs=(
            P(("patch", "exp"), "strip", "band"),
            P(("patch", "exp"), "strip", "band"),
            P(("patch", "exp"), "strip", None),
            P(("patch", "exp"), "strip", None),
            P(),
        ),
        out_specs=(P(("patch", "strip"), "band"), P(("patch", "exp"), "strip", "band")),
        check_vma=False,
    )
```

```python
import functools

import jax
import jax.numpy as jnp
from jax import lax
from jax.experimental import pallas as pl
from jax.experimental.pallas import tpu as pltpu
from jax.sharding import PartitionSpec as P

TILE_ROWS = 16
KERNEL = 9
GROUP = 3
RIM = KERNEL // 2
SLOTS = TILE_ROWS + 2 * RIM
LANES = 128
DEPTH = 256
SENTINEL = 1.0e30
LIMIT = 1.0e29
CHUNKS = 2

VMEM = pl.BlockSpec(memory_space=pltpu.VMEM)
SMEM = pl.BlockSpec(memory_space=pltpu.SMEM)


def call(body, outs, specs, flops, size, scratch=()):
    single = not isinstance(outs, (list, tuple))
    return pl.pallas_call(
        body,
        out_shape=outs,
        in_specs=specs,
        out_specs=VMEM if single else [VMEM] * len(outs),
        scratch_shapes=scratch,
        compiler_params=pltpu.CompilerParams(vmem_limit_bytes=12 << 20),
        cost_estimate=pl.CostEstimate(flops=flops, bytes_accessed=size, transcendentals=0),
    )


def iota(shape, dim):
    return lax.broadcasted_iota(jnp.int32, shape, dim)


def split(value):
    high = value.astype(jnp.bfloat16)
    low = (value - high.astype(jnp.float32)).astype(jnp.bfloat16)
    return high, low


def blend_row(col_count):
    columns = lax.axis_index("band") * col_count + iota((1, col_count), 1)
    return columns.astype(jnp.float32) / float(col_count * lax.axis_size("band") - 1)


def tap_rows(bank_ref):
    bank = bank_ref[...]
    normed = bank / jnp.sum(bank, axis=1, keepdims=True)
    tap = iota((KERNEL * KERNEL, DEPTH), 0)
    row_off = (tap * 57) >> 9
    col_off = tap - row_off * KERNEL
    place = (iota((KERNEL * KERNEL, DEPTH), 1) == col_off * SLOTS + row_off).astype(jnp.float32)
    first = jnp.dot(normed, place, precision=lax.Precision.HIGHEST, preferred_element_type=jnp.float32)
    lane = iota((TILE_ROWS, DEPTH), 1)
    slot = lane - SLOTS * ((lane * 2731) >> 16)
    for base in range(bank.shape[0]):
        spread = jnp.broadcast_to(first[base : base + 1], (TILE_ROWS, DEPTH))
        rows = pltpu.roll(spread, 0, 1, stride=1, stride_axis=0)
        yield base, jnp.where(slot < SLOTS - RIM, pltpu.roll(rows, DEPTH - RIM, 1), pltpu.roll(rows, SLOTS - RIM, 1))


def match_taps_body(bank_ref, index_ref, _, out_ref, all_ref):
    tiles, pair, count = index_ref.shape
    n = 2 * TILE_ROWS
    for base, rows in tap_rows(bank_ref):
        high, low = split(rows)
        all_ref[base, :TILE_ROWS, :] = high
        all_ref[base, TILE_ROWS:, :] = low
    for tile in range(tiles):
        for e in range(count):
            for k in range(pair):
                at = n * (2 * e + k)
                out_ref[tile, at : at + n, :] = all_ref[index_ref[tile, k, e]]


def warp_taps_body(bank_ref, index_ref, out_ref, all_ref):
    tiles, pair, count = index_ref.shape
    lane = iota((TILE_ROWS, DEPTH), 1)
    part = GROUP * SLOTS
    n = GROUP * TILE_ROWS
    for base, rows in tap_rows(bank_ref):
        high = rows.astype(jnp.bfloat16).astype(jnp.float32)
        low = rows - high
        turned = {(0, 0): high, (1, 0): low}

        def turn(which, steps):
            if (which, steps) not in turned:
                turned[which, steps] = pltpu.roll((high, low)[which], (part * steps) % DEPTH, 1)
            return turned[which, steps]

        for g in range(GROUP):
            value = jnp.where(lane < part, turn(0, -g), jnp.where(lane < 2 * part, turn(0, 1 - g), turn(1, 2 - g)))
            value = jnp.where(lane < 3 * part, value, 0.0)
            all_ref[base, g * TILE_ROWS : (g + 1) * TILE_ROWS, :] = value.astype(jnp.bfloat16)
    for tile in range(tiles):
        for e in range(count):
            for k in range(pair):
                out_ref[tile, e, k * n : (k + 1) * n, :] = all_ref[index_ref[tile, k, e]]


def shifted(rows):
    width = rows.shape[1]
    cols = width - LANES
    parts = []
    for col_off in range(KERNEL):
        amount = (RIM - col_off) % width
        moved = rows if amount == 0 else pltpu.roll(rows, amount, 1)
        parts.append(moved[:, :cols])
    parts.append(jnp.zeros((DEPTH - KERNEL * SLOTS, cols), jnp.float32))
    return split(jnp.concatenate(parts, axis=0))


def edge(first, last, has_first, has_last, lane):
    return jnp.where((lane < RIM) & has_first, first, 0.0) + jnp.where((lane >= LANES - RIM) & has_last, last, 0.0)


def sides():
    strip = lax.axis_index("strip")
    band = lax.axis_index("band")
    return (
        strip > 0,
        strip < lax.axis_size("strip") - 1,
        band > 0,
        band < lax.axis_size("band") - 1,
    )


def pack_body(swap_rows, swap_cols, images_ref, *outs):
    count, rows, cols = images_ref.shape
    above, below, left, right = sides()
    sub = iota((8, cols), 0)
    lane = iota((rows, LANES), 1)
    ups, downs = [], []
    for pair in range(count // 2):
        head = [images_ref[2 * pair + k, 0:8, :] for k in range(2)]
        tail = [images_ref[2 * pair + k, rows - 8 : rows, :] for k in range(2)]
        ups.append(jnp.where(sub < RIM, head[0], pltpu.roll(head[1], RIM, 0)))
        downs.append(jnp.where(sub < RIM, pltpu.roll(tail[0], RIM, 0), tail[1]))
    lefts = jnp.zeros((rows, LANES), jnp.float32)
    rights = jnp.zeros((rows, LANES), jnp.float32)
    for e in range(count):
        here = (lane >= RIM * e) & (lane < RIM * (e + 1))
        lefts = jnp.where(here, pltpu.roll(images_ref[e, :, :LANES], RIM * e, 1) if e else images_ref[e, :, :LANES], lefts)
        rights = jnp.where(here, pltpu.roll(images_ref[e, :, cols - LANES :], (RIM * (e + 1)) % LANES, 1), rights)
    outs = list(outs)
    if swap_rows:
        out = outs.pop(0)
        for pair in range(count // 2):
            out[8 * pair : 8 * pair + 8, :] = jnp.where(below, downs[pair], ups[pair])
    else:
        up, down = outs.pop(0), outs.pop(0)
        for pair in range(count // 2):
            up[8 * pair : 8 * pair + 8, :] = ups[pair]
            down[8 * pair : 8 * pair + 8, :] = downs[pair]
    if swap_cols:
        edges = [jnp.where(right, rights, lefts)]
    else:
        edges = [lefts, rights]
    for value in edges:
        outs.pop(0)[...] = value
    for value in edges:
        if swap_rows:
            outs.pop(0)[...] = jnp.where(below, value[rows - 8 :], value[:8])
        else:
            outs.pop(0)[...] = value[:8]
            outs.pop(0)[...] = value[rows - 8 :]


def warp_body(
    sent, blocks, images_ref, mask_ref, taps_ref, above_ref, below_ref, left_ref, right_ref, c_al, c_ar, c_bl, c_br, out_ref
):
    count, rows, cols = images_ref.shape
    tiles = rows // TILE_ROWS
    above, below, left, right = sides()
    parity = (lax.axis_index("exp") + lax.axis_index("strip")) % 2
    tile = (1 - parity) if sent else parity
    start = pl.multiple_of(tile * TILE_ROWS, TILE_ROWS)
    prior = pl.multiple_of(jnp.maximum(start - 8, 0), 8)
    after = pl.multiple_of(jnp.minimum(start + TILE_ROWS, rows - 8), 8)
    top = tile == 0
    end = tile == tiles - 1
    sub = iota((8, LANES), 0)
    lane = iota((SLOTS, LANES), 1)
    blend = blend_row(cols)
    width = 2 * LANES

    def side(ref, corner_above, corner_below):
        rim = jnp.where(
            sub < RIM,
            jnp.where(end, jnp.where(below, corner_below[...], 0.0), ref[pl.ds(after, 8), :]),
            jnp.where(top, jnp.where(above, corner_above[...], 0.0), ref[pl.ds(prior, 8), :]),
        )
        return jnp.concatenate([ref[pl.ds(start, TILE_ROWS), :], rim], axis=0)

    rights = jnp.where(right, side(right_ref, c_ar, c_br), 0.0)
    lefts = jnp.where(left, side(left_ref, c_al, c_bl), 0.0)
    last = cols // LANES - 1

    def source(e, block):
        if block < 0:
            return pltpu.roll(lefts, (LANES - RIM - RIM * e) % LANES, 1)
        if block > last:
            return pltpu.roll(rights, (LANES - RIM * e) % LANES, 1) if e else rights
        at = slice(block * LANES, (block + 1) * LANES)
        group = slice(8 * (e // 2), 8 * (e // 2) + 8)
        low_rows, high_rows = below_ref[group, at], above_ref[group, at]
        if e % 2:
            low_rows = pltpu.roll(low_rows, RIM, 0)
        else:
            high_rows = pltpu.roll(high_rows, RIM, 0)
        rim = jnp.where(
            sub < RIM,
            jnp.where(end, jnp.where(below, low_rows, 0.0), images_ref[e, pl.ds(after, 8), at]),
            jnp.where(top, jnp.where(above, high_rows, 0.0), images_ref[e, pl.ds(prior, 8), at]),
        )
        return jnp.concatenate([images_ref[e, pl.ds(start, TILE_ROWS), at], rim], axis=0)

    zero = jnp.zeros((DEPTH - 3 * GROUP * SLOTS, width), jnp.float32)
    for e in range(count):
        taps = taps_ref[tile, e]
        seen = {}

        def get(block):
            if block not in seen:
                seen[block] = source(e, block)
            return seen[block]

        for order, block in enumerate(blocks):
            rim = jnp.where(lane < RIM, get(block + 1), get(block - 1))
            field = jnp.concatenate([get(block), rim], axis=1)
            near = jnp.concatenate([pltpu.roll(field, 1, 1), field, pltpu.roll(field, width - 1, 1)], axis=0)
            high = near.astype(jnp.bfloat16).astype(jnp.float32)
            stack = jnp.concatenate([high, near - high, high, zero], axis=0).astype(jnp.bfloat16)
            sums = jnp.dot(taps, stack, preferred_element_type=jnp.float32)
            n = TILE_ROWS
            pair = []
            for k in range(2):
                at = k * GROUP * n
                pair.append(
                    pltpu.roll(sums[at : at + n], GROUP, 1)[:, :LANES]
                    + sums[at + n : at + 2 * n, :LANES]
                    + pltpu.roll(sums[at + 2 * n : at + 3 * n], width - GROUP, 1)[:, :LANES]
                )
            here = blend[:, block * LANES : (block + 1) * LANES]
            warped = (1.0 - here) * pair[0] + here * pair[1]
            valid = mask_ref[e, pl.ds(start, TILE_ROWS), block * LANES : (block + 1) * LANES] == 1
            out_ref[e, :, order * LANES : (order + 1) * LANES] = jnp.where(valid, warped, SENTINEL)


def insert_low(three, value):
    a, b, c = three
    over = jnp.maximum(a, value)
    a = jnp.minimum(a, value)
    more = jnp.maximum(b, over)
    b = jnp.minimum(b, over)
    return a, b, jnp.minimum(c, more)


def insert_high(three, value):
    a, b, c = three
    under = jnp.minimum(a, value)
    a = jnp.maximum(a, value)
    less = jnp.minimum(b, under)
    b = jnp.maximum(b, under)
    return a, b, jnp.maximum(c, less)


def odd_tile():
    return (lax.axis_index("exp") + lax.axis_index("strip")) % 2 == 1


def gather_body(first, edges, own_ref, other_ref, *refs):
    out_ref = refs[-2] if edges else refs[-1]
    count, rows, cols = other_ref.shape
    big = jnp.full((8, LANES), SENTINEL, jnp.float32)
    for r in range(0, rows, 8):
        for c in range(0, cols, LANES):
            total = jnp.zeros((8, LANES), jnp.float32)
            number = jnp.zeros((8, LANES), jnp.float32)
            low, high = (big, big, big), (-big, -big, -big)
            for ref, at in ((own_ref, c + first), (other_ref, c)):
                for e in range(count):
                    value = ref[e, r : r + 8, at : at + LANES]
                    valid = value < LIMIT
                    total = total + jnp.where(valid, value, 0.0)
                    number = number + jnp.where(valid, 1.0, 0.0)
                    low = insert_low(low, value)
                    high = insert_high(high, jnp.where(valid, value, -SENTINEL))
            for k, plane in enumerate((total, number) + low + high):
                out_ref[k, r : r + 8, c : c + LANES] = plane
    if edges:
        edge_rows(list(refs[:-2]) + [out_ref], refs[-1])


def edge_rows(states, edge_ref):
    odd = odd_tile()
    at = 0
    for ref in states:
        planes, rows, cols = ref.shape
        sub = iota((8, cols), 0)
        for p in range(planes // 2):
            head = [ref[2 * p + k, 0:8, :] for k in range(2)]
            tail = [ref[2 * p + k, rows - 8 : rows, :] for k in range(2)]
            even_value = jnp.where(sub < RIM, head[0], pltpu.roll(head[1], RIM, 0))
            odd_value = jnp.where(sub < RIM, pltpu.roll(tail[0], RIM, 0), tail[1])
            edge_ref[8 * p : 8 * p + 8, at : at + cols] = jnp.where(odd, odd_value, even_value)
        at += cols


def merge_low(a, b):
    return (
        jnp.minimum(a[0], b[0]),
        jnp.minimum(jnp.minimum(a[1], b[1]), jnp.maximum(a[0], b[0])),
        jnp.minimum(jnp.minimum(a[2], b[2]), jnp.minimum(jnp.maximum(a[1], b[0]), jnp.maximum(a[0], b[1]))),
    )


def merge_high(a, b):
    return (
        jnp.maximum(a[0], b[0]),
        jnp.maximum(jnp.maximum(a[1], b[1]), jnp.minimum(a[0], b[0])),
        jnp.maximum(jnp.maximum(a[2], b[2]), jnp.maximum(jnp.minimum(a[1], b[0]), jnp.minimum(a[0], b[1]))),
    )


def finish(a, b):
    total, number = a[0] + b[0], a[1] + b[1]
    low = merge_low(a[2:5], b[2:5])
    high = merge_high(a[5:8], b[5:8])
    low_sum = low[0] + low[1] + low[2]
    high_sum = high[0] + high[1] + high[2]
    return (total - low_sum - high_sum) / (number - 6.0)


def merge_body(edges, own_ref, other_ref, *refs):
    out_ref = refs[-2] if edges else refs[-1]
    _, rows, cols = own_ref.shape
    for r in range(0, rows, 8):
        for c in range(0, cols, LANES):
            a = [own_ref[k, r : r + 8, c : c + LANES] for k in range(8)]
            b = [other_ref[k, r : r + 8, c : c + LANES] for k in range(8)]
            planes = (a[0] + b[0], a[1] + b[1]) + merge_low(a[2:5], b[2:5]) + merge_high(a[5:8], b[5:8])
            for k, plane in enumerate(planes):
                out_ref[k, r : r + 8, c : c + LANES] = plane
    if edges:
        edge_rows(list(refs[:-2]) + [out_ref], refs[-1])


def final_body(_, near_ref, far_ref, *refs):
    *inputs, out_ref = refs
    rows = inputs[0].shape[1]
    at = 0
    for piece in range(len(inputs) // 2):
        own_ref, other_ref = inputs[2 * piece : 2 * piece + 2]
        for c in range(0, own_ref.shape[2], LANES):
            here = slice(at, at + LANES)
            at += LANES
            for r in range(0, rows, 8):
                both = [[ref[k, r : r + 8, c : c + LANES] for k in range(8)] for ref in (own_ref, other_ref)]
                out_ref[r : r + 8, here] = finish(*both)
            both = [
                [pltpu.roll(ref[k // 2 * 8 : k // 2 * 8 + 8, here], RIM, 0) if k % 2 else ref[k // 2 * 8 : k // 2 * 8 + 8, here] for k in range(8)]
                for ref in (near_ref, far_ref)
            ]
            value = finish(*both)
            out_ref[rows : rows + 8, here] = jnp.where(odd_tile(), value, pltpu.roll(value, RIM, 0))


def join_body(swap_cols, own_ref, pair_ref, coadd_ref, rim_ref, *outs):
    above, below, left, right = sides()
    even = ~odd_tile()
    own, pair = own_ref[...], pair_ref[...]
    n, cols = own.shape[0] - 8, own.shape[1]
    first, last = jnp.where(even, own, pair), jnp.where(even, pair, own)
    coadd_ref[:n, :] = first[:n]
    coadd_ref[n:, :] = last[:n]
    sub = iota((8, cols), 0)
    rim_ref[...] = jnp.where(sub < RIM, jnp.where(below, last[n:], 0.0), jnp.where(above, first[n:], 0.0))
    for ref, at in ((coadd_ref, 0), (rim_ref, 2 * n)):
        rows = ref.shape[0]
        lefts, rights = ref[:, :LANES], ref[:, cols - LANES :]
        if swap_cols:
            outs[0][at : at + rows, :] = jnp.where(right, rights, lefts)
        else:
            outs[0][at : at + rows, :] = lefts
            outs[1][at : at + rows, :] = rights


def match_body(images_ref, taps_ref, coadd_ref, rim_ref, left_ref, right_ref, coadd_out, out, out_ref, sems):
    count, rows, cols = images_ref.shape
    tiles = rows // TILE_ROWS
    whole = pltpu.make_async_copy(coadd_ref, coadd_out, sems.at[tiles])
    whole.start()
    _, _, left, right = sides()
    blend = blend_row(cols)
    sub = iota((8, cols), 0)
    lane = iota((rows + 8, LANES), 1)
    sub_l = iota((8, LANES), 0)
    edges = edge(right_ref[...], left_ref[...], right, left, lane)
    n = TILE_ROWS
    copies = []
    for tile in range(tiles):
        start = tile * n

        def rims(main, last, at):
            low = last if tile == tiles - 1 else main[start + n : start + n + 8]
            high = last if tile == 0 else main[start - 8 : start]
            return jnp.concatenate([main[start : start + n], jnp.where(at < RIM, low, high)], axis=0)

        body = rims(coadd_ref[...], rim_ref[...], sub)
        side = rims(edges[:rows], edges[rows:], sub_l)
        high, low = shifted(jnp.concatenate([body, side], axis=1))
        taps = taps_ref[tile]
        sums = jnp.dot(taps, high, preferred_element_type=jnp.float32) + jnp.dot(taps, low, preferred_element_type=jnp.float32)
        for e in range(count):
            at = 4 * n * e
            first = sums[at : at + n] + sums[at + n : at + 2 * n]
            second = sums[at + 2 * n : at + 3 * n] + sums[at + 3 * n : at + 4 * n]
            out_ref[tile, e] = images_ref[e, start : start + n, :] - ((1.0 - blend) * first + blend * second)
        copies.append(pltpu.make_async_copy(out_ref.at[tile], out.at[:, pl.ds(start, n), :], sems.at[tile]))
        copies[-1].start()
    for copy in copies:
        copy.wait()
    whole.wait()


def moved(value, exp_bit, strip_step, band_step):
    sizes = [lax.axis_size(a) for a in ("exp", "strip", "band")]
    pairs = []
    for z in range(sizes[0]):
        for s in range(sizes[1]):
            for b in range(sizes[2]):
                s_from, b_from = s + strip_step, b + band_step
                if sizes[1] == 2:
                    s_from %= 2
                if sizes[2] == 2:
                    b_from %= 2
                if 0 <= s_from < sizes[1] and 0 <= b_from < sizes[2]:
                    source = ((z ^ exp_bit) * sizes[1] + s_from) * sizes[2] + b_from
                    pairs.append((source, (z * sizes[1] + s) * sizes[2] + b))
    return lax.ppermute(value, ("exp", "strip", "band"), pairs)


def facing(value, exp_bit):
    sizes = [lax.axis_size(a) for a in ("exp", "strip", "band")]
    pairs = []
    for z in range(sizes[0]):
        for s in range(sizes[1]):
            s_from = s + (1 if (z + s) % 2 else -1)
            if sizes[1] % 2 == 0:
                s_from %= sizes[1]
            if 0 <= s_from < sizes[1]:
                for b in range(sizes[2]):
                    pairs.append((((z ^ exp_bit) * sizes[1] + s_from) * sizes[2] + b, (z * sizes[1] + s) * sizes[2] + b))
    return lax.ppermute(value, ("exp", "strip", "band"), pairs)


def on_device(images, valid_mask, basis_index, match_index, psf_bank):
    count, rows, cols = images.shape
    strips, bands, layers = lax.axis_size("strip"), lax.axis_size("band"), lax.axis_size("exp")
    swap_rows, swap_cols = strips == 2, bands == 2
    f32 = lambda *shape: jax.ShapeDtypeStruct(shape, jnp.float32)
    area = rows * cols

    row_outs = [f32(RIM * count, cols)] * (1 if swap_rows else 2)
    col_outs = [f32(rows, LANES)] * (1 if swap_cols else 2)
    corner_outs = [f32(8, LANES)] * (len(row_outs) * len(col_outs))
    packed = call(
        functools.partial(pack_body, swap_rows, swap_cols), row_outs + col_outs + corner_outs, [VMEM], 100000, 300000
    )(images)
    packed = list(packed)
    ups = [packed.pop(0) for _ in row_outs]
    edges = [packed.pop(0) for _ in col_outs]
    if swap_rows:
        above = below = moved(ups[0], 0, 1, 0)
    else:
        below, above = moved(ups[0], 0, 1, 0), moved(ups[1], 0, -1, 0)
    if swap_cols:
        left = right = moved(edges[0], 0, 0, 1)
    else:
        right, left = moved(edges[0], 0, 0, 1), moved(edges[1], 0, 0, -1)
    corners = {}
    for c in range(len(col_outs)):
        for r in range(len(row_outs)):
            value = packed.pop(0)
            corners[(r, c)] = moved(value, 0, 1 if r == 0 else -1, 1 if c == 0 else -1)
    at = lambda r, c: corners[(0 if swap_rows else r, 0 if swap_cols else c)]
    rims = (above, below, left, right, at(1, 1), at(1, 0), at(0, 1), at(0, 0))

    banks = psf_bank.shape[0]
    tiles = rows // TILE_ROWS
    turned = lambda index: jnp.transpose(index, (1, 2, 0))
    scratch = lambda n: [pltpu.VMEM((banks, n, DEPTH), jnp.bfloat16)]
    half = jnp.bfloat16
    warp_taps = call(
        warp_taps_body,
        jax.ShapeDtypeStruct((tiles, count, 2 * GROUP * TILE_ROWS, DEPTH), half),
        [VMEM, SMEM],
        10000000,
        300000,
        scratch(GROUP * TILE_ROWS),
    )(psf_bank, turned(basis_index))

    blocks = list(range(cols // LANES))
    pieces = [blocks] if CHUNKS == 1 else [[b] for b in blocks]

    def warp(sent, piece):
        return call(
            functools.partial(warp_body, sent, piece),
            f32(count, TILE_ROWS, LANES * len(piece)),
            [VMEM, VMEM, VMEM] + [VMEM] * 8,
            2 * TILE_ROWS * DEPTH * LANES * len(piece) * count * 12,
            1000000,
        )(images, valid_mask, warp_taps, *rims)

    sents = [moved(warp(True, piece), 1, 0, 0) for piece in pieces]
    own = warp(False, blocks)
    edge_out = f32(8 * RIM, cols)
    states = []
    for piece, sent in zip(pieces, sents):
        edges = layers == 4 and piece is pieces[-1]
        outs = f32(8, *sent.shape[1:])
        done = call(
            functools.partial(gather_body, LANES * piece[0], edges),
            [outs, edge_out] if edges else outs,
            [VMEM] * (2 + len(states) * edges),
            area * 100,
            400000,
        )(own, sent, *(states if edges else []))
        states.append(done[0] if edges else done)
        if edges:
            edge_state = done[1]
    match_taps = call(
        match_taps_body,
        jax.ShapeDtypeStruct((tiles, 4 * TILE_ROWS * count, DEPTH), half),
        [VMEM, SMEM, pl.BlockSpec(memory_space=pl.ANY)],
        10000000,
        300000,
        scratch(2 * TILE_ROWS),
    )(psf_bank, turned(match_index), states[0])
    bit = 2
    while 2 * bit < layers:
        others = [moved(state, bit, 0, 0) for state in states]
        before, states = states, []
        for own_state, other in zip(before, others):
            edges = 4 * bit == layers and own_state is before[-1]
            outs = f32(*other.shape)
            done = call(
                functools.partial(merge_body, edges),
                [outs, edge_out] if edges else outs,
                [VMEM] * (2 + len(states) * edges),
                area * 20,
                300000,
            )(own_state, other, *(states if edges else []))
            states.append(done[0] if edges else done)
            if edges:
                edge_state = done[1]
        bit *= 2
    others = [moved(state, bit, 0, 0) for state in states]
    near, far = facing(edge_state, 0), facing(edge_state, bit)
    group = [x for both in zip(states, others) for x in both]
    state = call(
        final_body,
        f32(TILE_ROWS + 8, cols),
        [pl.BlockSpec(memory_space=pl.ANY)] + [VMEM] * (2 + len(group)),
        area * 20,
        300000,
    )(match_taps, near, far, *group)
    pair = moved(state, 1, 0, 0)
    side_outs = [f32(rows + 8, LANES)] * (1 if swap_cols else 2)
    coadd, rim, *side = call(
        functools.partial(join_body, swap_cols), [f32(rows, cols), f32(8, cols)] + side_outs, [VMEM] * 2, 10000, 100000
    )(state, pair)
    if swap_cols:
        left = right = moved(side[0], 0, 0, 1)
    else:
        right, left = moved(side[0], 0, 0, 1), moved(side[1], 0, 0, -1)
    return pl.pallas_call(
        match_body,
        out_shape=[f32(rows, cols), f32(count, rows, cols)],
        in_specs=[VMEM] * 6,
        out_specs=[pl.BlockSpec(memory_space=pl.ANY)] * 2,
        scratch_shapes=[pltpu.VMEM((tiles, count, TILE_ROWS, cols), jnp.float32), pltpu.SemaphoreType.DMA((tiles + 1,))],
        compiler_params=pltpu.CompilerParams(vmem_limit_bytes=12 << 20),
        cost_estimate=pl.CostEstimate(flops=8 * area * DEPTH * count, bytes_accessed=1000000, transcendentals=0),
    )(images, match_taps, coadd, rim, left, right)


def solution(mesh):
    return jax.shard_map(
        on_device,
        mesh=mesh,
        in_specs=(
            P(("patch", "exp"), "strip", "band"),
            P(("patch", "exp"), "strip", "band"),
            P(("patch", "exp"), "strip", None),
            P(("patch", "exp"), "strip", None),
            P(),
        ),
        out_specs=(P(("patch", "strip"), "band"), P(("patch", "exp"), "strip", "band")),
        check_vma=False,
    )
```
